32 devices in a mesh: chan: 4 (over z), frame: 8 (over y, x, core).
Axes of the slice: x: 2, y: 2, z: 4, core: 2. Of those that a mesh axis runs over, the one named last changes fastest.
Arguments:
- rf_data: bfloat16 [2, 8, 256, 1024], P(None, None, 'frame', 'chan'), may hold values from -6 to 6
- elem_pos: int32 [3, 1024], replicated, may hold values from -16 to 15, as said below
- vox_pos: int32 [3, 4096], P(None, 'chan'), may hold values from -32 to 62, as said below
- subbands: int32 [8], replicated, may hold values from 0 to 63, as said below
Outputs:
- filtered: bfloat16 [256, 2, 8, 4096], P('frame', None, None, 'chan')
The draws below stay inside these ranges and needn't reach their ends.
Inputs may be any that keep to these rules, and one draw needn't show every extreme that they name: `elem_pos`: the element positions are the 32 x 32 grid with x and y from -16, each point once in a drawn order; z is 0, 1 or 2. `vox_pos`: distinct voxels of a box: x and y from -32 to 31, z from 48 to 62 in steps of 2. `subbands`: 8 distinct bin numbers.
All inputs are finite; a program needn't handle non-finite values.
Results may differ from the reference program's by a relative error of at most 0.0075.
Values may be sent and summed in bfloat16 or wider, within the bound.
A program may use at most 128 MiB of HBM per device.

```python
import math
import jax
import jax.numpy as jnp
from jax import lax

SIDE = 32
C = 1024
F = 256
B = 8
V = 4096


def draw_elem_pos(key, part):
    order = jax.random.permutation(jax.random.fold_in(key, 11), SIDE * SIDE).astype(jnp.int32)
    pos_x = order % SIDE - SIDE // 2
    pos_y = order // SIDE - SIDE // 2
    pos_z = jax.random.randint(jax.random.fold_in(key, 12), (SIDE * SIDE,), 0, 3).astype(jnp.int32)
    return jnp.stack([pos_x, pos_y, pos_z], axis=0).astype(jnp.int32)


def draw_vox_pos(key, part):
    middle = (jax.random.permutation(jax.random.fold_in(key, 21), 32766)[:V - 2] + 1).astype(jnp.int32)
    ends = jnp.array([0, 32767], dtype=jnp.int32)
    joined = jnp.concatenate([ends, middle]).astype(jnp.int32)
    chosen = jax.random.permutation(jax.random.fold_in(key, 22), joined).astype(jnp.int32)
    pos_x = chosen % 64 - 32
    pos_y = chosen // 64 % 64 - 32
    pos_z = 48 + 2 * (chosen // 4096)
    return jnp.stack([pos_x, pos_y, pos_z], axis=0).astype(jnp.int32)


def draw_subbands(key, part):
    middle = (jax.random.permutation(jax.random.fold_in(key, 31), 62)[:B - 2] + 1).astype(jnp.int32)
    ends = jnp.array([0, 63], dtype=jnp.int32)
    joined = jnp.concatenate([ends, middle]).astype(jnp.int32)
    return jax.random.permutation(jax.random.fold_in(key, 32), joined).astype(jnp.int32)


def block_scale(rng, dims, pieces, low, largest):
    level = 1.0
    for position, shards_of in pieces:
        draws = jax.random.uniform(jax.random.fold_in(jax.random.fold_in(rng, 6), position), (shards_of,), jnp.float32, low / len(pieces), largest / len(pieces))
        level = level * jnp.repeat(jnp.exp(draws), dims[position] // shards_of).reshape((-1,) + (1,) * (len(dims) - 1 - position))
    return level


def scatter_about(key, dims, width, bound, split=(), held_as=jnp.bfloat16):
    entries = jax.random.normal(key, dims, jnp.float32) * width
    if len(split) > 0:
        entries = block_scale(key, dims, split, -0.22, 0.18) * entries
    return jnp.clip(entries, min=-bound, max=bound).astype(held_as)


def setup_inputs(seed: int = 0) -> dict:
    splits = jax.random.split(jax.random.key(seed), 5)
    rf_data = scatter_about(splits[0], (2, B, F, C), 1.0, 6.0, ((2, 8), (3, 4)))
    elem_pos = draw_elem_pos(jax.random.fold_in(splits[4], 71), 0)
    vox_pos = draw_vox_pos(jax.random.fold_in(splits[4], 71), 0)
    subbands = draw_subbands(jax.random.fold_in(splits[4], 71), 0)
    return dict(rf_data=rf_data, elem_pos=elem_pos, vox_pos=vox_pos, subbands=subbands)


TWO_PI = 2.0 * math.pi
EPSILON = 1e-06

def geometry(elem_pos, vox_pos):
    elem = elem_pos.astype(jnp.float32)
    voxel = vox_pos.astype(jnp.float32)
    delta_x = voxel[0][:, None] - elem[0][None, :]
    delta_y = voxel[1][:, None] - elem[1][None, :]
    delta_z = voxel[2][:, None] - elem[2][None, :]
    distance = jnp.sqrt(delta_x * delta_x + delta_y * delta_y + delta_z * delta_z)
    inverse = 1.0 / math.sqrt(elem_pos.shape[1])
    weight = delta_z / distance * inverse
    travel = voxel[2][:, None] + distance
    return (weight, travel)

def data_matrix(rf_data):
    data_re = jnp.swapaxes(rf_data[0], 1, 2)
    data_im = jnp.swapaxes(rf_data[1], 1, 2)
    upper_rows = jnp.concatenate([data_re, data_im], axis=2)
    lower_rows = jnp.concatenate([-data_im, data_re], axis=2)
    return jnp.concatenate([upper_rows, lower_rows], axis=1)

def complex_product(left_pair, right_pair):
    first_re, first_im = left_pair
    second_re, second_im = right_pair
    high = lax.Precision.HIGHEST
    real_part = jnp.einsum('bij,bjk->bik', first_re, second_re, precision=high) - jnp.einsum('bij,bjk->bik', first_im, second_im, precision=high)
    imag_part = jnp.einsum('bij,bjk->bik', first_re, second_im, precision=high) + jnp.einsum('bij,bjk->bik', first_im, second_re, precision=high)
    return (real_part, imag_part)

def filter_matrix(gram):
    gram_re = gram[:, 0]
    gram_im = gram[:, 1]
    frames = gram.shape[2]
    squares = lax.optimization_barrier(jnp.sum(gram_re * gram_re + gram_im * gram_im, axis=(1, 2)))
    factor = 4.0 / jnp.sqrt(squares + EPSILON)
    mat_re = gram_re * factor[:, None, None]
    mat_im = gram_im * factor[:, None, None]
    second = complex_product((mat_re, mat_im), (mat_re, mat_im))
    third = complex_product(second, (mat_re, mat_im))
    identity = jnp.eye(frames, dtype=jnp.float32)[None]
    filter_re = identity - mat_re + 0.3 * second[0] - 0.03 * third[0]
    filter_im = -mat_im + 0.3 * second[1] - 0.03 * third[1]
    return jnp.stack([filter_re, filter_im], axis=1).astype(jnp.bfloat16)

def block_filter(filter_bf):
    filter_re = filter_bf[:, 0]
    filter_im = filter_bf[:, 1]
    upper_rows = jnp.concatenate([filter_re, filter_im], axis=2)
    lower_rows = jnp.concatenate([-filter_im, filter_re], axis=2)
    return jnp.concatenate([upper_rows, lower_rows], axis=1)

def reference(rf_data, elem_pos, vox_pos, subbands):
    weight, travel = geometry(elem_pos, vox_pos)
    wavenum = (32.0 + subbands.astype(jnp.float32)) / 64.0
    matrix = data_matrix(rf_data)

    def one_bin(index):
        phase_angle = TWO_PI * wavenum[index] * travel
        operator = jnp.concatenate([weight * jnp.cos(phase_angle), -(weight * jnp.sin(phase_angle))], axis=1).astype(jnp.bfloat16)
        return jnp.dot(operator, matrix[index], preferred_element_type=jnp.float32).astype(jnp.bfloat16)
    volumes = lax.map(one_bin, jnp.arange(B, dtype=jnp.int32))
    stacked = jnp.swapaxes(volumes, 0, 1).astype(jnp.float32)
    products = jnp.einsum('vbi,vbj->bij', stacked, stacked, precision=lax.Precision.HIGHEST)
    gram_re = products[:, :F, :F] + products[:, F:, F:]
    gram_im = products[:, :F, F:] - products[:, F:, :F]
    gram = jnp.stack([gram_re, gram_im], axis=1)
    filter_bf = filter_matrix(gram)
    blocks = block_filter(filter_bf).astype(jnp.float32)
    applied = jnp.einsum('vbi,bij->vbj', stacked, blocks, precision=lax.Precision.HIGHEST).astype(jnp.bfloat16)
    applied = applied.reshape(applied.shape[0], B, 2, F)
    return jnp.transpose(applied, (3, 2, 1, 0))
```

```python
import functools
import math

import jax
import jax.numpy as jnp
from jax import lax
from jax.experimental import pallas as pl
from jax.experimental.pallas import tpu as pltpu
from jax.sharding import PartitionSpec as P

EPSILON = 1e-06
MESH = pl.DeviceIdType.MESH
F32 = jnp.float32
BF16 = jnp.bfloat16
SIN_POLY = (
    3.1415927410125732, -5.167710304260254, 2.550077438354492,
    -0.598291277885437, 0.07765766233205795,
)
COS_POLY = (
    0.9999999403953552, -4.934792995452881, 4.058411121368408,
    -1.331876516342163, 0.21968960762023926,
)
LANES = 128
ROUND = 12582912.0


def horner(coefs, z):
    value = jnp.full_like(z, coefs[-1])
    for coef in coefs[-2::-1]:
        value = value * z + coef
    return value


def split(x):
    high = x.astype(BF16)
    return high, (x - high.astype(F32)).astype(BF16)


def dot(a, b):
    return jnp.dot(a, b, preferred_element_type=F32)


def dot_nt(a, b):
    return lax.dot_general(a, b, (((1,), (1,)), ((), ())), preferred_element_type=F32)


def kernel(
    nc, nf, nbins,
    rf_ref, elem_ref, vox_ref, sub_ref, out_ref,
    rfbuf, elem, vox, oper, acc, vols, part, slabs, total, sent,
    own_sem, plane_send, plane_recv, right_send, right_recv, left_send, left_recv,
    rs_send, rs_recv, ag_send, ag_recv, out_own, out_send, out_recv,
):
    share = nf // nbins
    frames = rfbuf.shape[2]
    cl = rfbuf.shape[3]
    chans = nc * cl
    vd = vols.shape[1]
    fl = frames // nf
    group = nc * share
    rows = frames // group
    me_c = lax.axis_index("chan")
    me_f = lax.axis_index("frame")
    me_bin = me_f // share
    me_sub = me_f % share
    me_g = me_c * share + me_sub

    def member(k):
        m = lax.rem(me_g + k, group)
        return m, (m // share, me_bin * share + m % share)

    def planar(k):
        j = lax.rem(me_f + k, nf)
        return j, (me_c, j)

    barrier = pltpu.get_barrier_semaphore()
    for k in range(1, nf):
        pl.semaphore_signal(barrier, inc=1, device_id=planar(k)[1], device_id_type=MESH)
    for k in range(1, nc):
        for s in range(share):
            other = (lax.rem(me_c + k, nc), me_bin * share + s)
            pl.semaphore_signal(barrier, inc=1, device_id=other, device_id_type=MESH)

    mine = pl.ds(pl.multiple_of(me_f * fl, fl), fl)
    own = pltpu.make_async_copy(rf_ref.at[:, me_bin], rfbuf.at[me_c, :, mine], own_sem)
    own.start()
    vstart = pl.multiple_of(me_sub * vd, LANES)
    vox[...] = vox_ref[:, pl.ds(vstart, vd)].astype(F32)
    for axis in range(3):
        for base in range(0, chans, LANES):
            row = elem_ref[axis:axis + 1, base:base + LANES].astype(F32)
            elem[axis, base:base + LANES, :] = jnp.broadcast_to(row, (LANES, LANES)).T
    pl.semaphore_wait(barrier, nf - 1 + (nc - 1) * share)

    def plane_copy(k):
        j, device = planar(k)
        return pltpu.make_async_remote_copy(
            src_ref=rf_ref.at[:, j // share], dst_ref=rfbuf.at[me_c, :, mine],
            send_sem=plane_send.at[j], recv_sem=plane_recv.at[me_f],
            device_id=device, device_id_type=MESH)

    def plane_arrival(k):
        j, device = planar(k)
        place = rfbuf.at[me_c, :, pl.ds(pl.multiple_of(j * fl, fl), fl)]
        return pltpu.make_async_remote_copy(
            src_ref=rf_ref.at[:, 0], dst_ref=place, send_sem=plane_send.at[j],
            recv_sem=plane_recv.at[j], device_id=device, device_id_type=MESH)

    for k in range(1, nf):
        plane_copy(k).start()

    wavenum = (32.0 + sub_ref[me_bin].astype(F32)) / 64.0
    inverse = 1.0 / math.sqrt(chans)

    def block_of(k):
        return lax.rem(me_c + k + nc, nc)

    def make_operator(block):
        @pl.loop(0, cl // 16)
        def _(step):
            place = pl.ds(pl.multiple_of(block * cl + step * 16, 16), 16)
            ex, ey, ez = elem[0, place, :], elem[1, place, :], elem[2, place, :]
            for base in range(0, vd, LANES):
                lanes = slice(base, base + LANES)
                vz = vox[2:3, lanes]
                dx, dy, dz = vox[0:1, lanes] - ex, vox[1:2, lanes] - ey, vz - ez
                square = dx * dx + dy * dy + dz * dz
                inv = lax.rsqrt(square)
                inv = inv * (1.5 - (0.5 * square) * (inv * inv))
                turns = wavenum * (vz + square * inv)
                turns = turns - ((turns + ROUND) - ROUND)
                z = turns * turns
                sine = turns * horner(SIN_POLY, z)
                cosine = horner(COS_POLY, z)
                weight = dz * inv * inverse
                twice = (weight + weight) * sine
                oper[0, place, lanes] = (weight - twice * sine).astype(BF16)
                oper[1, place, lanes] = (twice * cosine).astype(BF16)

    def multiply(block, first=False, last=False):
        place = pl.ds(pl.multiple_of(block * cl, cl), cl)
        real, imag = rfbuf[block, 0], rfbuf[block, 1]
        upper = jnp.concatenate([real, imag], axis=1)
        lower = jnp.concatenate([imag, -real], axis=1)
        width = min(256, vd)

        @pl.loop(0, vd // width)
        def _(step):
            lanes = pl.ds(pl.multiple_of(step * width, width), width)
            both = jnp.concatenate([oper[0, place, lanes], oper[1, place, lanes]], axis=0)
            for half, left in enumerate((upper, lower)):
                where = slice(half * frames, (half + 1) * frames)
                value = dot(left, both)
                if not first:
                    value = value + acc[where, lanes]
                if last:
                    vols[where, lanes] = value.astype(BF16)
                else:
                    acc[where, lanes] = value

    make_operator(me_c)
    own.wait()
    for k in range(1, nf):
        plane_arrival(k).wait_recv()

    right = (lax.rem(me_c + 1, nc), me_f)
    left = (lax.rem(me_c + nc - 1, nc), me_f)
    steps = nc // 2

    def ring_copy(step, rightward, arriving):
        sign = -1 if rightward else 1
        block = block_of(sign * (step if arriving else step - 1))
        ref = rfbuf.at[block]
        if step == steps:
            ref = rfbuf.at[block, 0 if rightward else 1]
        sends, recvs = (right_send, right_recv) if rightward else (left_send, left_recv)
        return pltpu.make_async_remote_copy(
            src_ref=ref, dst_ref=ref, send_sem=sends.at[step - 1], recv_sem=recvs.at[step - 1],
            device_id=right if rightward else left, device_id_type=MESH)

    for step in range(1, steps + 1):
        for rightward in (True, False):
            ring_copy(step, rightward, False).start()
        if step < steps:
            make_operator(block_of(-step))
            make_operator(block_of(step))
        else:
            make_operator(block_of(steps))
        if step == 1:
            multiply(me_c, first=True)
        else:
            multiply(block_of(1 - step))
            multiply(block_of(step - 1))
        for rightward in (True, False):
            ring_copy(step, rightward, True).wait_recv()
    multiply(block_of(steps), last=True)

    real, imag = vols[:frames, :], vols[frames:, :]
    both = jnp.concatenate([real, imag], axis=1)
    gram_re = dot_nt(both, both)
    gram_im = dot_nt(jnp.concatenate([real, -imag], axis=1), jnp.concatenate([imag, real], axis=1))
    across = lax.broadcasted_iota(jnp.int32, (frames, frames), 1)
    down = lax.broadcasted_iota(jnp.int32, (frames, frames), 0)
    part[...] = jnp.where(down <= across, gram_re, gram_im)

    def slab_of(m):
        return pl.ds(pl.multiple_of(m * rows, rows), rows)

    def scatter(k):
        m, device = member(k)
        return pltpu.make_async_remote_copy(
            src_ref=part.at[slab_of(m)], dst_ref=slabs.at[me_g],
            send_sem=rs_send.at[m], recv_sem=rs_recv.at[me_g],
            device_id=device, device_id_type=MESH)

    def scatter_arrival(k):
        m, device = member(k)
        return pltpu.make_async_remote_copy(
            src_ref=part.at[slab_of(m)], dst_ref=slabs.at[m],
            send_sem=rs_send.at[m], recv_sem=rs_recv.at[m],
            device_id=device, device_id_type=MESH)

    def gather(k, arriving=False):
        m, device = member(k)
        source = m if arriving else me_g
        return pltpu.make_async_remote_copy(
            src_ref=total.at[slab_of(source)], dst_ref=total.at[slab_of(source)],
            send_sem=ag_send.at[m], recv_sem=ag_recv.at[source],
            device_id=device, device_id_type=MESH)

    for k in range(1, group):
        scatter(k).start()
    summed = part[slab_of(me_g), :]
    for k in range(1, group):
        scatter_arrival(k).wait_recv()
        summed = summed + slabs[member(k)[0]]
    total[slab_of(me_g), :] = summed
    for k in range(1, group):
        gather(k).start()
    for k in range(1, group):
        gather(k, True).wait_recv()

    packed = total[...]
    turned = packed.T
    mat_re = jnp.where(down <= across, packed, turned)
    mat_im = jnp.where(down > across, packed, jnp.where(down < across, -turned, 0.0))
    squares = jnp.sum(jnp.sum(mat_re * mat_re + mat_im * mat_im, axis=1, keepdims=True), axis=0, keepdims=True)
    factor = 4.0 / jnp.sqrt(squares + EPSILON)
    mat_re = mat_re * factor
    mat_im = mat_im * factor
    rhs = jnp.concatenate(
        [jnp.concatenate([mat_re, mat_im], axis=1), jnp.concatenate([-mat_im, mat_re], axis=1)], axis=0)
    rhs_high, rhs_low = split(rhs)

    def product(pair):
        high, low = split(pair)
        return dot(high, rhs_high) + (dot(high, rhs_low) + dot(low, rhs_high))

    first = jnp.concatenate([mat_re, mat_im], axis=1)
    second = product(first)
    third = product(second)
    poly = 0.3 * second - 0.03 * third - first
    acc[:frames, :frames] = jnp.where(down == across, 1.0, 0.0) + poly[:, :frames]
    acc[frames:, :frames] = poly[:, frames:]

    def out_copy(j):
        return pltpu.make_async_remote_copy(
            src_ref=sent.at[:, pl.ds(pl.multiple_of(j * fl, fl), fl)], dst_ref=out_ref.at[me_f],
            send_sem=out_send.at[j], recv_sem=out_recv.at[me_f],
            device_id=(me_c, j), device_id_type=MESH)

    chunks = 4
    per = nf // chunks
    height = per * fl
    my_chunk = me_f // per
    for step in range(1, chunks + 1):
        chunk = lax.rem(my_chunk + step, chunks)
        place = pl.ds(pl.multiple_of(chunk * height, height), height)
        below = pl.ds(pl.multiple_of(frames + chunk * height, height), height)
        h_re = acc[place, :frames].astype(BF16)
        h_im = acc[below, :frames].astype(BF16)
        lhs = jnp.concatenate(
            [jnp.concatenate([h_re, h_im], axis=1), jnp.concatenate([-h_im, h_re], axis=1)], axis=0)
        value = dot(lhs, vols[...]).astype(BF16)
        sent[0, place, :] = value[:height]
        sent[1, place, :] = value[height:]
        for q in range(per):
            j = chunk * per + q
            if step < chunks:
                out_copy(j).start()
            else:
                @pl.when(j != me_f)
                def _():
                    out_copy(j).start()
    own_out = pltpu.make_async_copy(sent.at[:, mine], out_ref.at[me_f], out_own)
    own_out.start()
    for k in range(1, nf):
        plane_copy(k).wait_send()
    for step in range(1, steps + 1):
        for rightward in (True, False):
            ring_copy(step, rightward, False).wait_send()
    for k in range(1, group):
        scatter(k).wait_send()
        gather(k).wait_send()
    own_out.wait()
    for k in range(1, nf):
        j, device = planar(k)
        pltpu.make_async_remote_copy(
            src_ref=sent.at[:, mine], dst_ref=out_ref.at[j], send_sem=out_send.at[j],
            recv_sem=out_recv.at[j], device_id=device, device_id_type=MESH).wait()


def shards(nc, nf, rf_data, elem_pos, vox_pos, subbands):
    nbins, fl, cl = rf_data.shape[1:]
    frames = fl * nf
    chans = cl * nc
    share = nf // nbins
    vl = vox_pos.shape[1]
    vd = vl // share
    group = nc * share
    steps = nc // 2
    dma = pltpu.SemaphoreType.DMA
    vmem = pl.BlockSpec(memory_space=pltpu.VMEM)
    received = pl.pallas_call(
        functools.partial(kernel, nc, nf, nbins),
        out_shape=jax.ShapeDtypeStruct((nf, 2, fl, vd), BF16),
        in_specs=[vmem, vmem, vmem, pl.BlockSpec(memory_space=pltpu.SMEM)],
        out_specs=pl.BlockSpec(memory_space=pl.ANY),
        scratch_shapes=[
            pltpu.VMEM((nc, 2, frames, cl), BF16),
            pltpu.VMEM((3, chans, LANES), F32),
            pltpu.VMEM((3, vd), F32),
            pltpu.VMEM((2, chans, vd), BF16),
            pltpu.VMEM((2 * frames, vd), F32),
            pltpu.VMEM((2 * frames, vd), BF16),
            pltpu.VMEM((frames, frames), F32),
            pltpu.VMEM((group, frames // group, frames), F32),
            pltpu.VMEM((frames, frames), F32),
            pltpu.VMEM((2, frames, vd), BF16),
            dma, dma((nf,)), dma((nf,)),
            dma((steps,)), dma((steps,)), dma((steps,)), dma((steps,)),
            dma((group,)), dma((group,)), dma((group,)), dma((group,)),
            dma, dma((nf,)), dma((nf,)),
        ],
        compiler_params=pltpu.CompilerParams(
            collective_id=0, has_side_effects=True, vmem_limit_bytes=48 * 2**20),
    )(rf_data, elem_pos, vox_pos, subbands)
    received = received.reshape(nbins, share, 2, fl, vd)
    return jnp.transpose(received, (3, 2, 0, 1, 4)).reshape(fl, 2, nbins, vl)


def solution(mesh):
    return jax.shard_map(
        functools.partial(shards, mesh.shape["chan"], mesh.shape["frame"]),
        mesh=mesh,
        in_specs=(P(None, None, "frame", "chan"), P(), P(None, "chan"), P()),
        out_specs=P("frame", None, None, "chan"),
        check_vma=False,
    )
```

```python
import functools
import math

import jax
import jax.numpy as jnp
from jax import lax
from jax.experimental import pallas as pl
from jax.experimental.pallas import tpu as pltpu
from jax.sharding import PartitionSpec as P

EPSILON = 1e-06
MESH = pl.DeviceIdType.MESH
F32 = jnp.float32
BF16 = jnp.bfloat16
SIN_POLY = (
    3.1415927410125732, -5.167710304260254, 2.550077438354492,
    -0.598291277885437, 0.07765766233205795,
)
COS_POLY = (
    0.9999999403953552, -4.934792995452881, 4.058411121368408,
    -1.331876516342163, 0.21968960762023926,
)
LANES = 128
ROUND = 12582912.0


def horner(coefs, z):
    value = jnp.full_like(z, coefs[-1])
    for coef in coefs[-2::-1]:
        value = value * z + coef
    return value


def split(x):
    high = x.astype(BF16)
    return high, (x - high.astype(F32)).astype(BF16)


def dot(a, b):
    return jnp.dot(a, b, preferred_element_type=F32)


def dot_nt(a, b):
    return lax.dot_general(a, b, (((1,), (1,)), ((), ())), preferred_element_type=F32)


def kernel(
    nc, nf, nbins,
    rf_ref, elem_hbm, vox_hbm, sub_hbm, out_ref,
    rfbuf, elem_ref, vox_ref, sub_ref, in_sem, elem, vox, oper, acc, vols, part, slabs, total, sent,
    own_sem, plane_send, plane_recv, right_send, right_recv, left_send, left_recv,
    rs_send, rs_recv, ag_send, ag_recv, out_own, out_send, out_recv,
):
    share = nf // nbins
    frames = rfbuf.shape[2]
    cl = rfbuf.shape[3]
    chans = nc * cl
    vd = vols.shape[1]
    fl = frames // nf
    group = nc * share
    rows = frames // group
    me_c = lax.axis_index("chan")
    me_f = lax.axis_index("frame")
    me_bin = me_f // share
    me_sub = me_f % share
    me_g = me_c * share + me_sub

    def member(k):
        m = lax.rem(me_g + k, group)
        return m, (m // share, me_bin * share + m % share)

    def planar(k):
        j = lax.rem(me_f + k, nf)
        return j, (me_c, j)

    barrier = pltpu.get_barrier_semaphore()
    for k in range(1, nf):
        pl.semaphore_signal(barrier, inc=1, device_id=planar(k)[1], device_id_type=MESH)
    for k in range(1, nc):
        for s in range(share):
            other = (lax.rem(me_c + k, nc), me_bin * share + s)
            pl.semaphore_signal(barrier, inc=1, device_id=other, device_id_type=MESH)

    def piece(j):
        return pl.ds(pl.multiple_of(j * fl, fl), fl)

    mine = piece(me_f)
    own = pltpu.make_async_copy(rf_ref.at[:, me_bin], rfbuf.at[me_c, :, mine], own_sem)
    own.start()
    loads = [
        pltpu.make_async_copy(source, place, in_sem.at[index])
        for index, (source, place) in enumerate(
            ((elem_hbm, elem_ref), (vox_hbm, vox_ref), (sub_hbm, sub_ref)))
    ]
    for load in loads:
        load.start()
    own.wait()
    pl.semaphore_wait(barrier, nf - 1 + (nc - 1) * share)

    def plane_copy(k):
        j, device = planar(k)
        return pltpu.make_async_remote_copy(
            src_ref=rf_ref.at[:, j // share], dst_ref=rfbuf.at[me_c, :, mine],
            send_sem=plane_send.at[j], recv_sem=plane_recv.at[me_f],
            device_id=device, device_id_type=MESH)

    def plane_arrival(j):
        return pltpu.make_async_remote_copy(
            src_ref=rf_ref.at[:, 0], dst_ref=rfbuf.at[me_c, :, piece(j)], send_sem=plane_send.at[j],
            recv_sem=plane_recv.at[j], device_id=(me_c, j), device_id_type=MESH)

    for k in range(1, nf):
        plane_copy(k).start()

    inverse = 1.0 / math.sqrt(chans)

    def block_of(k):
        return lax.rem(me_c + k + nc, nc)

    def make_operator(block, offset, count):
        @pl.loop(0, count)
        def _(step):
            place = pl.ds(pl.multiple_of(block * cl + (offset + step) * 16, 16), 16)
            ex, ey, ez = elem[0, place, :], elem[1, place, :], elem[2, place, :]
            for base in range(0, vd, LANES):
                lanes = slice(base, base + LANES)
                vz = vox[2:3, lanes]
                dx, dy, dz = vox[0:1, lanes] - ex, vox[1:2, lanes] - ey, vz - ez
                square = dx * dx + dy * dy + dz * dz
                inv = lax.rsqrt(square)
                inv = inv * (1.5 - (0.5 * square) * (inv * inv))
                turns = wavenum * (vz + square * inv)
                turns = turns - ((turns + ROUND) - ROUND)
                z = turns * turns
                sine = turns * horner(SIN_POLY, z)
                cosine = horner(COS_POLY, z)
                weight = dz * inv * inverse
                twice = (weight + weight) * sine
                oper[0, place, lanes] = (weight - twice * sine).astype(BF16)
                oper[1, place, lanes] = (twice * cosine).astype(BF16)

    def multiply(block, first=False, last=False):
        place = pl.ds(pl.multiple_of(block * cl, cl), cl)
        real, imag = rfbuf[block, 0], rfbuf[block, 1]
        upper = jnp.concatenate([real, imag], axis=1)
        lower = jnp.concatenate([imag, -real], axis=1)
        width = min(256, vd)

        @pl.loop(0, vd // width)
        def _(step):
            lanes = pl.ds(pl.multiple_of(step * width, width), width)
            both = jnp.concatenate([oper[0, place, lanes], oper[1, place, lanes]], axis=0)
            for half, left in enumerate((upper, lower)):
                where = slice(half * frames, (half + 1) * frames)
                value = dot(left, both)
                if not first:
                    value = value + acc[where, lanes]
                if last:
                    vols[where, lanes] = value.astype(BF16)
                else:
                    acc[where, lanes] = value

    right = (lax.rem(me_c + 1, nc), me_f)
    left = (lax.rem(me_c + nc - 1, nc), me_f)
    steps = nc // 2

    def ring_copy(step, j, rightward, arriving):
        sign = -1 if rightward else 1
        block = block_of(sign * (step if arriving else step - 1))
        ref = rfbuf.at[block, :, piece(j)]
        if step == steps:
            ref = rfbuf.at[block, 0 if rightward else 1, piece(j)]
        sends, recvs = (right_send, right_recv) if rightward else (left_send, left_recv)
        index = (step - 1) * nf + j
        return pltpu.make_async_remote_copy(
            src_ref=ref, dst_ref=ref, send_sem=sends.at[index], recv_sem=recvs.at[index],
            device_id=right if rightward else left, device_id_type=MESH)

    for rightward in (True, False):
        ring_copy(1, me_f, rightward, False).start()

    for load in loads:
        load.wait()
    vstart = pl.multiple_of(me_sub * vd, LANES)
    vox[...] = vox_ref[:, pl.ds(vstart, vd)].astype(F32)
    for axis in range(3):
        for base in range(0, chans, LANES):
            row = elem_ref[axis:axis + 1, base:base + LANES].astype(F32)
            elem[axis, base:base + LANES, :] = jnp.broadcast_to(row, (LANES, LANES)).T
    wavenum = (32.0 + sub_ref[me_bin].astype(F32)) / 64.0

    tall = cl // 16
    portion = 2 * tall // nf

    def portion_of_operator(phase, k):
        at = k * portion
        later = at >= tall
        block = jnp.where(later, block_of(-phase - 1), block_of(phase))
        make_operator(block, jnp.where(later, at - tall, at), portion)

    portion_of_operator(0, 0)

    @pl.loop(1, nf)
    def _(k):
        j = lax.rem(me_f - k + nf, nf)
        plane_arrival(j).wait_recv()
        for rightward in (True, False):
            ring_copy(1, j, rightward, False).start()
        portion_of_operator(0, k)

    for step in range(1, steps):
        if step == 1:
            multiply(me_c, first=True)
        else:
            multiply(block_of(1 - step))
            multiply(block_of(step - 1))

        @pl.loop(0, nf)
        def _(k):
            j = lax.rem(me_f - k + nf, nf)
            for rightward in (True, False):
                ring_copy(step, j, rightward, True).wait_recv()
                ring_copy(step + 1, j, rightward, False).start()
            portion_of_operator(step, k)

    if steps == 1:
        multiply(me_c, first=True)
    else:
        multiply(block_of(1 - steps))
        multiply(block_of(steps - 1))

    @pl.loop(0, nf)
    def _(k):
        j = lax.rem(me_f - k + nf, nf)
        for rightward in (True, False):
            ring_copy(steps, j, rightward, True).wait_recv()

    multiply(block_of(steps), last=True)

    real, imag = vols[:frames, :], vols[frames:, :]
    both = jnp.concatenate([real, imag], axis=1)
    gram_re = dot_nt(both, both)
    gram_im = dot_nt(jnp.concatenate([real, -imag], axis=1), jnp.concatenate([imag, real], axis=1))
    across = lax.broadcasted_iota(jnp.int32, (frames, frames), 1)
    down = lax.broadcasted_iota(jnp.int32, (frames, frames), 0)
    part[...] = jnp.where(down <= across, gram_re, gram_im).astype(BF16)

    def slab_of(m):
        return pl.ds(pl.multiple_of(m * rows, rows), rows)

    def scatter(k):
        m, device = member(k)
        return pltpu.make_async_remote_copy(
            src_ref=part.at[slab_of(m)], dst_ref=slabs.at[me_g],
            send_sem=rs_send.at[m], recv_sem=rs_recv.at[me_g],
            device_id=device, device_id_type=MESH)

    def scatter_arrival(k):
        m, device = member(k)
        return pltpu.make_async_remote_copy(
            src_ref=part.at[slab_of(m)], dst_ref=slabs.at[m],
            send_sem=rs_send.at[m], recv_sem=rs_recv.at[m],
            device_id=device, device_id_type=MESH)

    def gather(k, arriving=False):
        m, device = member(k)
        source = m if arriving else me_g
        return pltpu.make_async_remote_copy(
            src_ref=total.at[slab_of(source)], dst_ref=total.at[slab_of(source)],
            send_sem=ag_send.at[m], recv_sem=ag_recv.at[source],
            device_id=device, device_id_type=MESH)

    for k in range(1, group):
        scatter(k).start()
    summed = part[slab_of(me_g), :].astype(F32)
    for k in range(1, group):
        scatter_arrival(k).wait_recv()
        summed = summed + slabs[member(k)[0]].astype(F32)
    total[slab_of(me_g), :] = summed.astype(BF16)
    for k in range(1, group):
        gather(k).start()
    for k in range(1, group):
        gather(k, True).wait_recv()

    packed = total[...].astype(F32)
    turned = packed.T
    mat_re = jnp.where(down <= across, packed, turned)
    mat_im = jnp.where(down > across, packed, jnp.where(down < across, -turned, 0.0))
    squares = jnp.sum(jnp.sum(mat_re * mat_re + mat_im * mat_im, axis=1, keepdims=True), axis=0, keepdims=True)
    factor = 4.0 / jnp.sqrt(squares + EPSILON)
    mat_re = mat_re * factor
    mat_im = mat_im * factor
    rhs = jnp.concatenate(
        [jnp.concatenate([mat_re, mat_im], axis=1), jnp.concatenate([-mat_im, mat_re], axis=1)], axis=0)
    rhs_high, rhs_low = split(rhs)

    def product(pair):
        high, low = split(pair)
        return dot(high, rhs_high) + (dot(high, rhs_low) + dot(low, rhs_high))

    first = jnp.concatenate([mat_re, mat_im], axis=1)
    second = product(first)
    third = product(second)
    poly = 0.3 * second - 0.03 * third - first
    acc[:frames, :frames] = jnp.where(down == across, 1.0, 0.0) + poly[:, :frames]
    acc[frames:, :frames] = poly[:, frames:]

    def out_copy(j):
        return pltpu.make_async_remote_copy(
            src_ref=sent.at[:, pl.ds(pl.multiple_of(j * fl, fl), fl)], dst_ref=out_ref.at[me_f],
            send_sem=out_send.at[j], recv_sem=out_recv.at[me_f],
            device_id=(me_c, j), device_id_type=MESH)

    chunks = 4
    per = nf // chunks
    height = per * fl
    my_chunk = me_f // per
    for step in range(1, chunks + 1):
        chunk = lax.rem(my_chunk + step, chunks)
        place = pl.ds(pl.multiple_of(chunk * height, height), height)
        below = pl.ds(pl.multiple_of(frames + chunk * height, height), height)
        h_re = acc[place, :frames].astype(BF16)
        h_im = acc[below, :frames].astype(BF16)
        lhs = jnp.concatenate(
            [jnp.concatenate([h_re, h_im], axis=1), jnp.concatenate([-h_im, h_re], axis=1)], axis=0)
        value = dot(lhs, vols[...]).astype(BF16)
        sent[0, place, :] = value[:height]
        sent[1, place, :] = value[height:]
        for q in range(per):
            j = chunk * per + q
            if step < chunks:
                out_copy(j).start()
            else:
                @pl.when(j != me_f)
                def _():
                    out_copy(j).start()
    own_out = pltpu.make_async_copy(sent.at[:, mine], out_ref.at[me_f], out_own)
    own_out.start()
    for k in range(1, nf):
        plane_copy(k).wait_send()
    for step in range(1, steps + 1):
        @pl.loop(0, nf)
        def _(j):
            for rightward in (True, False):
                ring_copy(step, j, rightward, False).wait_send()

    for k in range(1, group):
        scatter(k).wait_send()
        gather(k).wait_send()
    own_out.wait()
    for k in range(1, nf):
        j, device = planar(k)
        pltpu.make_async_remote_copy(
            src_ref=sent.at[:, mine], dst_ref=out_ref.at[j], send_sem=out_send.at[j],
            recv_sem=out_recv.at[j], device_id=device, device_id_type=MESH).wait()


def shards(nc, nf, rf_data, elem_pos, vox_pos, subbands):
    nbins, fl, cl = rf_data.shape[1:]
    frames = fl * nf
    chans = cl * nc
    share = nf // nbins
    vl = vox_pos.shape[1]
    vd = vl // share
    group = nc * share
    steps = nc // 2
    dma = pltpu.SemaphoreType.DMA
    received = pl.pallas_call(
        functools.partial(kernel, nc, nf, nbins),
        out_shape=jax.ShapeDtypeStruct((nf, 2, fl, vd), BF16),
        in_specs=[pl.BlockSpec(memory_space=pl.ANY)] * 4,
        out_specs=pl.BlockSpec(memory_space=pl.ANY),
        scratch_shapes=[
            pltpu.VMEM((nc, 2, frames, cl), BF16),
            pltpu.VMEM(elem_pos.shape, elem_pos.dtype),
            pltpu.VMEM(vox_pos.shape, vox_pos.dtype),
            pltpu.SMEM(subbands.shape, subbands.dtype),
            dma((3,)),
            pltpu.VMEM((3, chans, LANES), F32),
            pltpu.VMEM((3, vd), F32),
            pltpu.VMEM((2, chans, vd), BF16),
            pltpu.VMEM((2 * frames, vd), F32),
            pltpu.VMEM((2 * frames, vd), BF16),
            pltpu.VMEM((frames, frames), BF16),
            pltpu.VMEM((group, frames // group, frames), BF16),
            pltpu.VMEM((frames, frames), BF16),
            pltpu.VMEM((2, frames, vd), BF16),
            dma, dma((nf,)), dma((nf,)),
            dma((steps * nf,)), dma((steps * nf,)), dma((steps * nf,)), dma((steps * nf,)),
            dma((group,)), dma((group,)), dma((group,)), dma((group,)),
            dma, dma((nf,)), dma((nf,)),
        ],
        compiler_params=pltpu.CompilerParams(
            collective_id=0, has_side_effects=True, vmem_limit_bytes=60 * 2**20),
    )(rf_data, elem_pos, vox_pos, subbands)
    received = received.reshape(nbins, share, 2, fl, vd)
    return jnp.transpose(received, (3, 2, 0, 1, 4)).reshape(fl, 2, nbins, vl)


def solution(mesh):
    return jax.shard_map(
        functools.partial(shards, mesh.shape["chan"], mesh.shape["frame"]),
        mesh=mesh,
        in_specs=(P(None, None, "frame", "chan"), P(), P(None, "chan"), P()),
        out_specs=P("frame", None, None, "chan"),
        check_vma=False,
    )
```

```python
import functools
import math

import jax
import jax.numpy as jnp
from jax import lax
from jax.experimental import pallas as pl
from jax.experimental.pallas import tpu as pltpu
from jax.sharding import PartitionSpec as P

EPSILON = 1e-06
MESH = pl.DeviceIdType.MESH
F32 = jnp.float32
BF16 = jnp.bfloat16
SIN_POLY = (
    3.1415927410125732, -5.167710304260254, 2.550077438354492,
    -0.598291277885437, 0.07765766233205795,
)
COS_POLY = (
    0.9999999403953552, -4.934792995452881, 4.058411121368408,
    -1.331876516342163, 0.21968960762023926,
)
LANES = 128
ROUND = 12582912.0
GO_AT = 4


def horner(coefs, z):
    value = jnp.full_like(z, coefs[-1])
    for coef in coefs[-2::-1]:
        value = value * z + coef
    return value


def split(x):
    high = x.astype(BF16)
    return high, (x - high.astype(F32)).astype(BF16)


def dot(a, b):
    return jnp.dot(a, b, preferred_element_type=F32)


def dot_nt(a, b):
    return lax.dot_general(a, b, (((1,), (1,)), ((), ())), preferred_element_type=F32)


def kernel(
    nc, nf, nbins,
    rf_ref, elem_hbm, vox_hbm, sub_hbm, out_ref,
    rfbuf, elem_ref, vox_ref, sub_ref, in_sem, elem, vox, oper, acc, vols, part, slabs, total, sent,
    go_sem, own_sem, plane_send, plane_recv, right_send, right_recv, left_send, left_recv,
    rs_send, rs_recv, ag_send, ag_recv, out_own, out_send, out_recv,
):
    share = nf // nbins
    frames = rfbuf.shape[2]
    cl = rfbuf.shape[3]
    chans = nc * cl
    vd = vols.shape[1]
    fl = frames // nf
    group = nc * share
    rows = frames // group
    me_c = lax.axis_index("chan")
    me_f = lax.axis_index("frame")
    me_bin = me_f // share
    me_sub = me_f % share
    me_g = me_c * share + me_sub

    def member(k):
        m = lax.rem(me_g + k, group)
        return m, (m // share, me_bin * share + m % share)

    def planar(k):
        j = lax.rem(me_f + k, nf)
        return j, (me_c, j)

    barrier = pltpu.get_barrier_semaphore()
    for k in range(1, nf):
        pl.semaphore_signal(barrier, inc=1, device_id=planar(k)[1], device_id_type=MESH)
    for k in range(1, nc):
        for s in range(share):
            other = (lax.rem(me_c + k, nc), me_bin * share + s)
            pl.semaphore_signal(barrier, inc=1, device_id=other, device_id_type=MESH)

    def piece(j):
        return pl.ds(pl.multiple_of(j * fl, fl), fl)

    mine = piece(me_f)
    own = pltpu.make_async_copy(rf_ref.at[:, me_bin], rfbuf.at[me_c, :, mine], own_sem)
    own.start()
    loads = [
        pltpu.make_async_copy(source, place, in_sem.at[index])
        for index, (source, place) in enumerate(
            ((elem_hbm, elem_ref), (vox_hbm, vox_ref), (sub_hbm, sub_ref)))
    ]
    for load in loads:
        load.start()
    own.wait()
    pl.semaphore_wait(barrier, nf - 1 + (nc - 1) * share)

    def plane_copy(k):
        j, device = planar(k)
        return pltpu.make_async_remote_copy(
            src_ref=rf_ref.at[:, j // share], dst_ref=rfbuf.at[me_c, :, mine],
            send_sem=plane_send.at[j], recv_sem=plane_recv.at[me_f],
            device_id=device, device_id_type=MESH)

    def plane_arrival(j):
        return pltpu.make_async_remote_copy(
            src_ref=rf_ref.at[:, 0], dst_ref=rfbuf.at[me_c, :, piece(j)], send_sem=plane_send.at[j],
            recv_sem=plane_recv.at[j], device_id=(me_c, j), device_id_type=MESH)

    for k in range(1, nf):
        plane_copy(k).start()

    inverse = 1.0 / math.sqrt(chans)

    def block_of(k):
        return lax.rem(me_c + k + nc, nc)

    def make_operator(block, offset, count):
        @pl.loop(0, count)
        def _(step):
            place = pl.ds(pl.multiple_of(block * cl + (offset + step) * 16, 16), 16)
            ex, ey, ez = elem[0, place, :], elem[1, place, :], elem[2, place, :]
            for base in range(0, vd, LANES):
                lanes = slice(base, base + LANES)
                vz = vox[2:3, lanes]
                dx, dy, dz = vox[0:1, lanes] - ex, vox[1:2, lanes] - ey, vz - ez
                square = dx * dx + dy * dy + dz * dz
                inv = lax.rsqrt(square)
                inv = inv * (1.5 - (0.5 * square) * (inv * inv))
                turns = wavenum * (vz + square * inv)
                turns = turns - ((turns + ROUND) - ROUND)
                z = turns * turns
                sine = turns * horner(SIN_POLY, z)
                cosine = horner(COS_POLY, z)
                weight = dz * inv * inverse
                twice = (weight + weight) * sine
                oper[0, place, lanes] = (weight - twice * sine).astype(BF16)
                oper[1, place, lanes] = (twice * cosine).astype(BF16)

    def multiply(block, first=False, last=False):
        place = pl.ds(pl.multiple_of(block * cl, cl), cl)
        real, imag = rfbuf[block, 0], rfbuf[block, 1]
        upper = jnp.concatenate([real, imag], axis=1)
        lower = jnp.concatenate([imag, -real], axis=1)
        width = min(256, vd)

        @pl.loop(0, vd // width)
        def _(step):
            lanes = pl.ds(pl.multiple_of(step * width, width), width)
            both = jnp.concatenate([oper[0, place, lanes], oper[1, place, lanes]], axis=0)
            for half, left in enumerate((upper, lower)):
                where = slice(half * frames, (half + 1) * frames)
                value = dot(left, both)
                if not first:
                    value = value + acc[where, lanes]
                if last:
                    vols[where, lanes] = value.astype(BF16)
                else:
                    acc[where, lanes] = value

    right = (lax.rem(me_c + 1, nc), me_f)
    left = (lax.rem(me_c + nc - 1, nc), me_f)
    steps = nc // 2

    def ring_copy(step, j, rightward, arriving):
        sign = -1 if rightward else 1
        block = block_of(sign * (step if arriving else step - 1))
        ref = rfbuf.at[block, :, piece(j)]
        if step == steps:
            ref = rfbuf.at[block, 0 if rightward else 1, piece(j)]
        sends, recvs = (right_send, right_recv) if rightward else (left_send, left_recv)
        index = (step - 1) * nf + j
        return pltpu.make_async_remote_copy(
            src_ref=ref, dst_ref=ref, send_sem=sends.at[index], recv_sem=recvs.at[index],
            device_id=right if rightward else left, device_id_type=MESH)

    stagger = share == 1 and nf % 2 == 0
    second = lax.rem(me_f, 2) == 1

    def unless_second(run):
        if stagger:
            pl.when(jnp.logical_not(second))(run)
        else:
            run()

    def send_own():
        for rightward in (True, False):
            ring_copy(1, me_f, rightward, False).start()

    def let_go():
        pl.semaphore_signal(go_sem, inc=1, device_id=(me_c, me_f + 1), device_id_type=MESH)

    unless_second(send_own)
    for load in loads:
        load.wait()
    vstart = pl.multiple_of(me_sub * vd, LANES)
    vox[...] = vox_ref[:, pl.ds(vstart, vd)].astype(F32)
    for axis in range(3):
        for base in range(0, chans, LANES):
            row = elem_ref[axis:axis + 1, base:base + LANES].astype(F32)
            elem[axis, base:base + LANES, :] = jnp.broadcast_to(row, (LANES, LANES)).T
    wavenum = (32.0 + sub_ref[me_bin].astype(F32)) / 64.0

    tall = cl // 16
    portion = 2 * tall // nf

    def portion_of_operator(phase, k):
        at = k * portion
        later = at >= tall
        block = jnp.where(later, block_of(-phase - 1), block_of(phase))
        make_operator(block, jnp.where(later, at - tall, at), portion)

    if stagger:
        @pl.when(second)
        def _():
            make_operator(0, 0, nc * tall)
            pl.semaphore_wait(go_sem, 1)
            send_own()

    unless_second(lambda: portion_of_operator(0, 0))

    @pl.loop(1, nf)
    def _(k):
        j = lax.rem(me_f - k + nf, nf)
        plane_arrival(j).wait_recv()
        for rightward in (True, False):
            ring_copy(1, j, rightward, False).start()
        unless_second(lambda: portion_of_operator(0, k))

    if stagger and steps == 1:
        unless_second(let_go)

    for step in range(1, steps):
        if step == 1:
            multiply(me_c, first=True)
        else:
            multiply(block_of(1 - step))
            multiply(block_of(step - 1))

        @pl.loop(0, nf)
        def _(k):
            j = lax.rem(me_f - k + nf, nf)
            for rightward in (True, False):
                ring_copy(step, j, rightward, True).wait_recv()
                ring_copy(step + 1, j, rightward, False).start()
            if stagger and step == steps - 1:
                @pl.when(jnp.logical_and(jnp.logical_not(second), k == GO_AT * nf // 8))
                def _():
                    let_go()

            unless_second(lambda: portion_of_operator(step, k))

    if steps == 1:
        multiply(me_c, first=True)
    else:
        multiply(block_of(1 - steps))
        multiply(block_of(steps - 1))

    @pl.loop(0, nf)
    def _(k):
        j = lax.rem(me_f - k + nf, nf)
        for rightward in (True, False):
            ring_copy(steps, j, rightward, True).wait_recv()

    multiply(block_of(steps), last=True)

    real, imag = vols[:frames, :], vols[frames:, :]
    both = jnp.concatenate([real, imag], axis=1)
    gram_re = dot_nt(both, both)
    gram_im = dot_nt(jnp.concatenate([real, -imag], axis=1), jnp.concatenate([imag, real], axis=1))
    across = lax.broadcasted_iota(jnp.int32, (frames, frames), 1)
    down = lax.broadcasted_iota(jnp.int32, (frames, frames), 0)
    part[...] = jnp.where(down <= across, gram_re, gram_im).astype(BF16)

    def slab_of(m):
        return pl.ds(pl.multiple_of(m * rows, rows), rows)

    def scatter(k):
        m, device = member(k)
        return pltpu.make_async_remote_copy(
            src_ref=part.at[slab_of(m)], dst_ref=slabs.at[me_g],
            send_sem=rs_send.at[m], recv_sem=rs_recv.at[me_g],
            device_id=device, device_id_type=MESH)

    def scatter_arrival(k):
        m, device = member(k)
        return pltpu.make_async_remote_copy(
            src_ref=part.at[slab_of(m)], dst_ref=slabs.at[m],
            send_sem=rs_send.at[m], recv_sem=rs_recv.at[m],
            device_id=device, device_id_type=MESH)

    def gather(k, arriving=False):
        m, device = member(k)
        source = m if arriving else me_g
        return pltpu.make_async_remote_copy(
            src_ref=total.at[slab_of(source)], dst_ref=total.at[slab_of(source)],
            send_sem=ag_send.at[m], recv_sem=ag_recv.at[source],
            device_id=device, device_id_type=MESH)

    for k in range(1, group):
        scatter(k).start()
    summed = part[slab_of(me_g), :].astype(F32)
    for k in range(1, group):
        scatter_arrival(k).wait_recv()
        summed = summed + slabs[member(k)[0]].astype(F32)
    total[slab_of(me_g), :] = summed.astype(BF16)
    for k in range(1, group):
        gather(k).start()
    for k in range(1, group):
        gather(k, True).wait_recv()

    packed = total[...].astype(F32)
    turned = packed.T
    mat_re = jnp.where(down <= across, packed, turned)
    mat_im = jnp.where(down > across, packed, jnp.where(down < across, -turned, 0.0))
    squares = jnp.sum(jnp.sum(mat_re * mat_re + mat_im * mat_im, axis=1, keepdims=True), axis=0, keepdims=True)
    factor = 4.0 / jnp.sqrt(squares + EPSILON)
    mat_re = mat_re * factor
    mat_im = mat_im * factor
    rhs = jnp.concatenate(
        [jnp.concatenate([mat_re, mat_im], axis=1), jnp.concatenate([-mat_im, mat_re], axis=1)], axis=0)
    rhs_high, rhs_low = split(rhs)

    def product(pair):
        high, low = split(pair)
        return dot(high, rhs_high) + (dot(high, rhs_low) + dot(low, rhs_high))

    first = jnp.concatenate([mat_re, mat_im], axis=1)
    second = product(first)
    third = product(second)
    poly = 0.3 * second - 0.03 * third - first
    acc[:frames, :frames] = jnp.where(down == across, 1.0, 0.0) + poly[:, :frames]
    acc[frames:, :frames] = poly[:, frames:]

    def out_copy(j):
        return pltpu.make_async_remote_copy(
            src_ref=sent.at[:, pl.ds(pl.multiple_of(j * fl, fl), fl)], dst_ref=out_ref.at[me_f],
            send_sem=out_send.at[j], recv_sem=out_recv.at[me_f],
            device_id=(me_c, j), device_id_type=MESH)

    chunks = 4
    per = nf // chunks
    height = per * fl
    my_chunk = me_f // per
    for step in range(1, chunks + 1):
        chunk = lax.rem(my_chunk + step, chunks)
        place = pl.ds(pl.multiple_of(chunk * height, height), height)
        below = pl.ds(pl.multiple_of(frames + chunk * height, height), height)
        h_re = acc[place, :frames].astype(BF16)
        h_im = acc[below, :frames].astype(BF16)
        lhs = jnp.concatenate(
            [jnp.concatenate([h_re, h_im], axis=1), jnp.concatenate([-h_im, h_re], axis=1)], axis=0)
        value = dot(lhs, vols[...]).astype(BF16)
        sent[0, place, :] = value[:height]
        sent[1, place, :] = value[height:]
        for q in range(per):
            j = chunk * per + q
            if step < chunks:
                out_copy(j).start()
            else:
                @pl.when(j != me_f)
                def _():
                    out_copy(j).start()
    own_out = pltpu.make_async_copy(sent.at[:, mine], out_ref.at[me_f], out_own)
    own_out.start()
    for k in range(1, nf):
        plane_copy(k).wait_send()
    for step in range(1, steps + 1):
        @pl.loop(0, nf)
        def _(j):
            for rightward in (True, False):
                ring_copy(step, j, rightward, False).wait_send()

    for k in range(1, group):
        scatter(k).wait_send()
        gather(k).wait_send()
    own_out.wait()
    for k in range(1, nf):
        j, device = planar(k)
        pltpu.make_async_remote_copy(
            src_ref=sent.at[:, mine], dst_ref=out_ref.at[j], send_sem=out_send.at[j],
            recv_sem=out_recv.at[j], device_id=device, device_id_type=MESH).wait()


def shards(nc, nf, rf_data, elem_pos, vox_pos, subbands):
    nbins, fl, cl = rf_data.shape[1:]
    frames = fl * nf
    chans = cl * nc
    share = nf // nbins
    vl = vox_pos.shape[1]
    vd = vl // share
    group = nc * share
    steps = nc // 2
    dma = pltpu.SemaphoreType.DMA
    received = pl.pallas_call(
        functools.partial(kernel, nc, nf, nbins),
        out_shape=jax.ShapeDtypeStruct((nf, 2, fl, vd), BF16),
        in_specs=[pl.BlockSpec(memory_space=pl.ANY)] * 4,
        out_specs=pl.BlockSpec(memory_space=pl.ANY),
        scratch_shapes=[
            pltpu.VMEM((nc, 2, frames, cl), BF16),
            pltpu.VMEM(elem_pos.shape, elem_pos.dtype),
            pltpu.VMEM(vox_pos.shape, vox_pos.dtype),
            pltpu.SMEM(subbands.shape, subbands.dtype),
            dma((3,)),
            pltpu.VMEM((3, chans, LANES), F32),
            pltpu.VMEM((3, vd), F32),
            pltpu.VMEM((2, chans, vd), BF16),
            pltpu.VMEM((2 * frames, vd), F32),
            pltpu.VMEM((2 * frames, vd), BF16),
            pltpu.VMEM((frames, frames), BF16),
            pltpu.VMEM((group, frames // group, frames), BF16),
            pltpu.VMEM((frames, frames), BF16),
            pltpu.VMEM((2, frames, vd), BF16),
            pltpu.SemaphoreType.REGULAR, dma, dma((nf,)), dma((nf,)),
            dma((steps * nf,)), dma((steps * nf,)), dma((steps * nf,)), dma((steps * nf,)),
            dma((group,)), dma((group,)), dma((group,)), dma((group,)),
            dma, dma((nf,)), dma((nf,)),
        ],
        compiler_params=pltpu.CompilerParams(
            collective_id=0, has_side_effects=True, vmem_limit_bytes=60 * 2**20),
    )(rf_data, elem_pos, vox_pos, subbands)
    received = received.reshape(nbins, share, 2, fl, vd)
    return jnp.transpose(received, (3, 2, 0, 1, 4)).reshape(fl, 2, nbins, vl)


def solution(mesh):
    return jax.shard_map(
        functools.partial(shards, mesh.shape["chan"], mesh.shape["frame"]),
        mesh=mesh,
        in_specs=(P(None, None, "frame", "chan"), P(), P(None, "chan"), P()),
        out_specs=P("frame", None, None, "chan"),
        check_vma=False,
    )
```

```python
import functools
import math

import jax
import jax.numpy as jnp
from jax import lax
from jax.experimental import pallas as pl
from jax.experimental.pallas import tpu as pltpu
from jax.sharding import PartitionSpec as P

EPSILON = 1e-06
MESH = pl.DeviceIdType.MESH
F32 = jnp.float32
BF16 = jnp.bfloat16
SIN_POLY = (
    3.1415927410125732, -5.167710304260254, 2.550077438354492,
    -0.598291277885437, 0.07765766233205795,
)
COS_POLY = (
    0.9999999403953552, -4.934792995452881, 4.058411121368408,
    -1.331876516342163, 0.21968960762023926,
)
LANES = 128
ROUND = 12582912.0
GO_AT = 7


def horner(coefs, z):
    value = jnp.full_like(z, coefs[-1])
    for coef in coefs[-2::-1]:
        value = value * z + coef
    return value


def split(x):
    high = x.astype(BF16)
    return high, (x - high.astype(F32)).astype(BF16)


def dot(a, b):
    return jnp.dot(a, b, preferred_element_type=F32)


def dot_nt(a, b):
    return lax.dot_general(a, b, (((1,), (1,)), ((), ())), preferred_element_type=F32)


def kernel(
    nc, nf, nbins,
    rf_ref, elem_hbm, vox_hbm, sub_hbm, out_ref,
    rfbuf, elem_ref, vox_ref, sub_ref, in_sem, elem, vox, oper, acc, vols, part, slabs, total, sent,
    go_sem, own_sem, plane_send, plane_recv, right_send, right_recv, left_send, left_recv,
    rs_send, rs_recv, ag_send, ag_recv, out_own, out_send, out_recv,
):
    share = nf // nbins
    frames = rfbuf.shape[2]
    cl = rfbuf.shape[3]
    chans = nc * cl
    vd = vols.shape[1]
    fl = frames // nf
    group = nc * share
    rows = frames // group
    me_c = lax.axis_index("chan")
    me_f = lax.axis_index("frame")
    me_bin = me_f // share
    me_sub = me_f % share
    me_g = me_c * share + me_sub

    def member(k):
        m = lax.rem(me_g + k, group)
        return m, (m // share, me_bin * share + m % share)

    def planar(k):
        j = lax.rem(me_f + k, nf)
        return j, (me_c, j)

    barrier = pltpu.get_barrier_semaphore()
    for k in range(1, nf):
        pl.semaphore_signal(barrier, inc=1, device_id=planar(k)[1], device_id_type=MESH)
    for k in range(1, nc):
        for s in range(share):
            other = (lax.rem(me_c + k, nc), me_bin * share + s)
            pl.semaphore_signal(barrier, inc=1, device_id=other, device_id_type=MESH)

    def piece(j):
        return pl.ds(pl.multiple_of(j * fl, fl), fl)

    mine = piece(me_f)
    own = pltpu.make_async_copy(rf_ref.at[:, me_bin], rfbuf.at[me_c, :, mine], own_sem)
    own.start()
    loads = [
        pltpu.make_async_copy(source, place, in_sem.at[index])
        for index, (source, place) in enumerate(
            ((elem_hbm, elem_ref), (vox_hbm, vox_ref), (sub_hbm, sub_ref)))
    ]
    for load in loads:
        load.start()
    own.wait()
    pl.semaphore_wait(barrier, nf - 1 + (nc - 1) * share)

    def plane_copy(k):
        j, device = planar(k)
        return pltpu.make_async_remote_copy(
            src_ref=rf_ref.at[:, j // share], dst_ref=rfbuf.at[me_c, :, mine],
            send_sem=plane_send.at[j], recv_sem=plane_recv.at[me_f],
            device_id=device, device_id_type=MESH)

    def plane_arrival(j):
        return pltpu.make_async_remote_copy(
            src_ref=rf_ref.at[:, 0], dst_ref=rfbuf.at[me_c, :, piece(j)], send_sem=plane_send.at[j],
            recv_sem=plane_recv.at[j], device_id=(me_c, j), device_id_type=MESH)

    for k in range(1, nf):
        plane_copy(k).start()

    inverse = 1.0 / math.sqrt(chans)

    def block_of(k):
        return lax.rem(me_c + k + nc, nc)

    def make_operator(block, offset, count):
        @pl.loop(0, count)
        def _(step):
            place = pl.ds(pl.multiple_of(block * cl + (offset + step) * 16, 16), 16)
            ex, ey, ez = elem[0, place, :], elem[1, place, :], elem[2, place, :]
            for base in range(0, vd, LANES):
                lanes = slice(base, base + LANES)
                vz = vox[2:3, lanes]
                dx, dy, dz = vox[0:1, lanes] - ex, vox[1:2, lanes] - ey, vz - ez
                square = dx * dx + dy * dy + dz * dz
                inv = lax.rsqrt(square)
                inv = inv * (1.5 - (0.5 * square) * (inv * inv))
                turns = wavenum * (vz + square * inv)
                turns = turns - ((turns + ROUND) - ROUND)
                z = turns * turns
                sine = turns * horner(SIN_POLY, z)
                cosine = horner(COS_POLY, z)
                weight = dz * inv * inverse
                twice = (weight + weight) * sine
                oper[0, place, lanes] = (weight - twice * sine).astype(BF16)
                oper[1, place, lanes] = (twice * cosine).astype(BF16)

    def multiply(block, first=False, last=False):
        place = pl.ds(pl.multiple_of(block * cl, cl), cl)
        real, imag = rfbuf[block, 0], rfbuf[block, 1]
        upper = jnp.concatenate([real, imag], axis=1)
        lower = jnp.concatenate([imag, -real], axis=1)
        width = min(256, vd)

        @pl.loop(0, vd // width)
        def _(step):
            lanes = pl.ds(pl.multiple_of(step * width, width), width)
            both = jnp.concatenate([oper[0, place, lanes], oper[1, place, lanes]], axis=0)
            for half, left in enumerate((upper, lower)):
                where = slice(half * frames, (half + 1) * frames)
                value = dot(left, both)
                if not first:
                    value = value + acc[where, lanes]
                if last:
                    vols[where, lanes] = value.astype(BF16)
                else:
                    acc[where, lanes] = value

    right = (lax.rem(me_c + 1, nc), me_f)
    left = (lax.rem(me_c + nc - 1, nc), me_f)
    steps = nc // 2

    def ring_copy(step, j, rightward, arriving):
        sign = -1 if rightward else 1
        block = block_of(sign * (step if arriving else step - 1))
        ref = rfbuf.at[block, :, piece(j)]
        if step == steps:
            ref = rfbuf.at[block, 0 if rightward else 1, piece(j)]
        sends, recvs = (right_send, right_recv) if rightward else (left_send, left_recv)
        index = (step - 1) * nf + j
        return pltpu.make_async_remote_copy(
            src_ref=ref, dst_ref=ref, send_sem=sends.at[index], recv_sem=recvs.at[index],
            device_id=right if rightward else left, device_id_type=MESH)

    stagger = share == 1 and nf % 2 == 0
    second = lax.rem(me_f, 2) == 1

    def unless_second(run):
        if stagger:
            pl.when(jnp.logical_not(second))(run)
        else:
            run()

    def send_own():
        for rightward in (True, False):
            ring_copy(1, me_f, rightward, False).start()

    def let_go():
        pl.semaphore_signal(go_sem, inc=1, device_id=(me_c, me_f + 1), device_id_type=MESH)

    unless_second(send_own)
    for load in loads:
        load.wait()
    vstart = pl.multiple_of(me_sub * vd, LANES)
    vox[...] = vox_ref[:, pl.ds(vstart, vd)].astype(F32)
    for axis in range(3):
        for base in range(0, chans, LANES):
            row = elem_ref[axis:axis + 1, base:base + LANES].astype(F32)
            elem[axis, base:base + LANES, :] = jnp.broadcast_to(row, (LANES, LANES)).T
    wavenum = (32.0 + sub_ref[me_bin].astype(F32)) / 64.0

    tall = cl // 16
    portion = 2 * tall // nf

    def portion_of_operator(phase, k):
        at = k * portion
        later = at >= tall
        block = jnp.where(later, block_of(-phase - 1), block_of(phase))
        make_operator(block, jnp.where(later, at - tall, at), portion)

    if stagger:
        @pl.when(second)
        def _():
            make_operator(0, 0, nc * tall)
            pl.semaphore_wait(go_sem, 1)
            send_own()

    unless_second(lambda: portion_of_operator(0, 0))

    @pl.loop(1, nf)
    def _(k):
        j = lax.rem(me_f - k + nf, nf)
        plane_arrival(j).wait_recv()
        for rightward in (True, False):
            ring_copy(1, j, rightward, False).start()
        unless_second(lambda: portion_of_operator(0, k))

    if stagger and steps == 1:
        unless_second(let_go)

    for step in range(1, steps):
        if step == 1:
            multiply(me_c, first=True)
        else:
            multiply(block_of(1 - step))
            multiply(block_of(step - 1))

        @pl.loop(0, nf)
        def _(k):
            j = lax.rem(me_f - k + nf, nf)
            for rightward in (True, False):
                ring_copy(step, j, rightward, True).wait_recv()
                ring_copy(step + 1, j, rightward, False).start()
            if stagger and step == steps - 1:
                @pl.when(jnp.logical_and(jnp.logical_not(second), k == GO_AT * nf // 8))
                def _():
                    let_go()

            unless_second(lambda: portion_of_operator(step, k))

    if steps == 1:
        multiply(me_c, first=True)
    else:
        multiply(block_of(1 - steps))
        multiply(block_of(steps - 1))

    @pl.loop(0, nf)
    def _(k):
        j = lax.rem(me_f - k + nf, nf)
        for rightward in (True, False):
            ring_copy(steps, j, rightward, True).wait_recv()

    multiply(block_of(steps), last=True)

    real, imag = vols[:frames, :], vols[frames:, :]
    both = jnp.concatenate([real, imag], axis=1)
    gram_re = dot_nt(both, both)
    gram_im = dot_nt(jnp.concatenate([real, -imag], axis=1), jnp.concatenate([imag, real], axis=1))
    across = lax.broadcasted_iota(jnp.int32, (frames, frames), 1)
    down = lax.broadcasted_iota(jnp.int32, (frames, frames), 0)
    part[...] = jnp.where(down <= across, gram_re, gram_im).astype(BF16)

    def slab_of(m):
        return pl.ds(pl.multiple_of(m * rows, rows), rows)

    def scatter(k):
        m, device = member(k)
        return pltpu.make_async_remote_copy(
            src_ref=part.at[slab_of(m)], dst_ref=slabs.at[me_g],
            send_sem=rs_send.at[m], recv_sem=rs_recv.at[me_g],
            device_id=device, device_id_type=MESH)

    def scatter_arrival(k):
        m, device = member(k)
        return pltpu.make_async_remote_copy(
            src_ref=part.at[slab_of(m)], dst_ref=slabs.at[m],
            send_sem=rs_send.at[m], recv_sem=rs_recv.at[m],
            device_id=device, device_id_type=MESH)

    def gather(k, arriving=False):
        m, device = member(k)
        source = m if arriving else me_g
        return pltpu.make_async_remote_copy(
            src_ref=total.at[slab_of(source)], dst_ref=total.at[slab_of(source)],
            send_sem=ag_send.at[m], recv_sem=ag_recv.at[source],
            device_id=device, device_id_type=MESH)

    for k in range(1, group):
        scatter(k).start()
    summed = part[slab_of(me_g), :].astype(F32)
    for k in range(1, group):
        scatter_arrival(k).wait_recv()
        summed = summed + slabs[member(k)[0]].astype(F32)
    total[slab_of(me_g), :] = summed.astype(BF16)
    for k in range(1, group):
        gather(k).start()
    for k in range(1, group):
        gather(k, True).wait_recv()

    packed = total[...].astype(F32)
    turned = packed.T
    mat_re = jnp.where(down <= across, packed, turned)
    mat_im = jnp.where(down > across, packed, jnp.where(down < across, -turned, 0.0))
    squares = jnp.sum(jnp.sum(mat_re * mat_re + mat_im * mat_im, axis=1, keepdims=True), axis=0, keepdims=True)
    factor = 4.0 / jnp.sqrt(squares + EPSILON)
    mat_re = mat_re * factor
    mat_im = mat_im * factor
    rhs = jnp.concatenate(
        [jnp.concatenate([mat_re, mat_im], axis=1), jnp.concatenate([-mat_im, mat_re], axis=1)], axis=0)
    rhs_high, rhs_low = split(rhs)

    def product(pair):
        high, low = split(pair)
        return dot(high, rhs_high) + (dot(high, rhs_low) + dot(low, rhs_high))

    first = jnp.concatenate([mat_re, mat_im], axis=1)
    second = product(first)
    third = product(second)
    poly = 0.3 * second - 0.03 * third - first
    acc[:frames, :frames] = jnp.where(down == across, 1.0, 0.0) + poly[:, :frames]
    acc[frames:, :frames] = poly[:, frames:]

    def out_copy(j):
        return pltpu.make_async_remote_copy(
            src_ref=sent.at[:, pl.ds(pl.multiple_of(j * fl, fl), fl)], dst_ref=out_ref.at[me_f],
            send_sem=out_send.at[j], recv_sem=out_recv.at[me_f],
            device_id=(me_c, j), device_id_type=MESH)

    chunks = 4
    per = nf // chunks
    height = per * fl
    my_chunk = me_f // per
    for step in range(1, chunks + 1):
        chunk = lax.rem(my_chunk + step, chunks)
        place = pl.ds(pl.multiple_of(chunk * height, height), height)
        below = pl.ds(pl.multiple_of(frames + chunk * height, height), height)
        h_re = acc[place, :frames].astype(BF16)
        h_im = acc[below, :frames].astype(BF16)
        lhs = jnp.concatenate(
            [jnp.concatenate([h_re, h_im], axis=1), jnp.concatenate([-h_im, h_re], axis=1)], axis=0)
        value = dot(lhs, vols[...]).astype(BF16)
        sent[0, place, :] = value[:height]
        sent[1, place, :] = value[height:]
        for q in range(per):
            j = chunk * per + q
            if step < chunks:
                out_copy(j).start()
            else:
                @pl.when(j != me_f)
                def _():
                    out_copy(j).start()
    own_out = pltpu.make_async_copy(sent.at[:, mine], out_ref.at[me_f], out_own)
    own_out.start()
    for k in range(1, nf):
        plane_copy(k).wait_send()
    for step in range(1, steps + 1):
        @pl.loop(0, nf)
        def _(j):
            for rightward in (True, False):
                ring_copy(step, j, rightward, False).wait_send()

    for k in range(1, group):
        scatter(k).wait_send()
        gather(k).wait_send()
    own_out.wait()
    for k in range(1, nf):
        j, device = planar(k)
        pltpu.make_async_remote_copy(
            src_ref=sent.at[:, mine], dst_ref=out_ref.at[j], send_sem=out_send.at[j],
            recv_sem=out_recv.at[j], device_id=device, device_id_type=MESH).wait()


def shards(nc, nf, rf_data, elem_pos, vox_pos, subbands):
    nbins, fl, cl = rf_data.shape[1:]
    frames = fl * nf
    chans = cl * nc
    share = nf // nbins
    vl = vox_pos.shape[1]
    vd = vl // share
    group = nc * share
    steps = nc // 2
    dma = pltpu.SemaphoreType.DMA
    received = pl.pallas_call(
        functools.partial(kernel, nc, nf, nbins),
        out_shape=jax.ShapeDtypeStruct((nf, 2, fl, vd), BF16),
        in_specs=[pl.BlockSpec(memory_space=pl.ANY)] * 4,
        out_specs=pl.BlockSpec(memory_space=pl.ANY),
        scratch_shapes=[
            pltpu.VMEM((nc, 2, frames, cl), BF16),
            pltpu.VMEM(elem_pos.shape, elem_pos.dtype),
            pltpu.VMEM(vox_pos.shape, vox_pos.dtype),
            pltpu.SMEM(subbands.shape, subbands.dtype),
            dma((3,)),
            pltpu.VMEM((3, chans, LANES), F32),
            pltpu.VMEM((3, vd), F32),
            pltpu.VMEM((2, chans, vd), BF16),
            pltpu.VMEM((2 * frames, vd), F32),
            pltpu.VMEM((2 * frames, vd), BF16),
            pltpu.VMEM((frames, frames), BF16),
            pltpu.VMEM((group, frames // group, frames), BF16),
            pltpu.VMEM((frames, frames), BF16),
            pltpu.VMEM((2, frames, vd), BF16),
            pltpu.SemaphoreType.REGULAR, dma, dma((nf,)), dma((nf,)),
            dma((steps * nf,)), dma((steps * nf,)), dma((steps * nf,)), dma((steps * nf,)),
            dma((group,)), dma((group,)), dma((group,)), dma((group,)),
            dma, dma((nf,)), dma((nf,)),
        ],
        compiler_params=pltpu.CompilerParams(
            collective_id=0, has_side_effects=True, vmem_limit_bytes=60 * 2**20),
    )(rf_data, elem_pos, vox_pos, subbands)
    received = received.reshape(nbins, share, 2, fl, vd)
    return jnp.transpose(received, (3, 2, 0, 1, 4)).reshape(fl, 2, nbins, vl)


def solution(mesh):
    return jax.shard_map(
        functools.partial(shards, mesh.shape["chan"], mesh.shape["frame"]),
        mesh=mesh,
        in_specs=(P(None, None, "frame", "chan"), P(), P(None, "chan"), P()),
        out_specs=P("frame", None, None, "chan"),
        check_vma=False,
    )
```

```python
import functools
import math

import jax
import jax.numpy as jnp
from jax import lax
from jax.experimental import pallas as pl
from jax.experimental.pallas import tpu as pltpu
from jax.sharding import PartitionSpec as P

EPSILON = 1e-06
MESH = pl.DeviceIdType.MESH
F32 = jnp.float32
BF16 = jnp.bfloat16
SIN_POLY = (
    3.1415927410125732, -5.167710304260254, 2.550077438354492,
    -0.598291277885437, 0.07765766233205795,
)
COS_POLY = (
    0.9999999403953552, -4.934792995452881, 4.058411121368408,
    -1.331876516342163, 0.21968960762023926,
)
LANES = 128
ROUND = 12582912.0
GO_AT = 7


def horner(coefs, z):
    value = jnp.full_like(z, coefs[-1])
    for coef in coefs[-2::-1]:
        value = value * z + coef
    return value


def split(x):
    high = x.astype(BF16)
    return high, (x - high.astype(F32)).astype(BF16)


def dot(a, b):
    return jnp.dot(a, b, preferred_element_type=F32)


def dot_nt(a, b):
    return lax.dot_general(a, b, (((1,), (1,)), ((), ())), preferred_element_type=F32)


def kernel(
    nc, nf, nbins,
    rf_ref, elem_hbm, vox_hbm, sub_hbm, out_ref,
    rfbuf, elem_ref, vox_ref, sub_ref, in_sem, elem, vox, oper, acc, vols, part, slabs, total, sent,
    go_sem, own_sem, plane_send, plane_recv, right_send, right_recv, left_send, left_recv,
    rs_send, rs_recv, ag_send, ag_recv, out_own, out_send, out_recv,
):
    share = nf // nbins
    frames = rfbuf.shape[2]
    cl = rfbuf.shape[3]
    chans = nc * cl
    vd = vols.shape[1]
    fl = frames // nf
    group = nc * share
    rows = frames // group
    me_c = lax.axis_index("chan")
    me_f = lax.axis_index("frame")
    me_bin = me_f // share
    me_sub = me_f % share
    me_g = me_c * share + me_sub

    def member(k):
        m = lax.rem(me_g + k, group)
        return m, (m // share, me_bin * share + m % share)

    def planar(k):
        j = lax.rem(me_f + k, nf)
        return j, (me_c, j)

    barrier = pltpu.get_barrier_semaphore()
    for k in range(1, nf):
        pl.semaphore_signal(barrier, inc=1, device_id=planar(k)[1], device_id_type=MESH)
    for k in range(1, nc):
        for s in range(share):
            other = (lax.rem(me_c + k, nc), me_bin * share + s)
            pl.semaphore_signal(barrier, inc=1, device_id=other, device_id_type=MESH)

    def piece(j):
        return pl.ds(pl.multiple_of(j * fl, fl), fl)

    mine = piece(me_f)
    own = pltpu.make_async_copy(rf_ref.at[:, me_bin], rfbuf.at[me_c, :, mine], own_sem)
    own.start()
    loads = [
        pltpu.make_async_copy(source, place, in_sem.at[index])
        for index, (source, place) in enumerate(
            ((elem_hbm, elem_ref), (vox_hbm, vox_ref), (sub_hbm, sub_ref)))
    ]
    for load in loads:
        load.start()
    own.wait()
    pl.semaphore_wait(barrier, nf - 1 + (nc - 1) * share)

    def plane_copy(k):
        j, device = planar(k)
        return pltpu.make_async_remote_copy(
            src_ref=rf_ref.at[:, j // share], dst_ref=rfbuf.at[me_c, :, mine],
            send_sem=plane_send.at[j], recv_sem=plane_recv.at[me_f],
            device_id=device, device_id_type=MESH)

    def plane_arrival(j):
        return pltpu.make_async_remote_copy(
            src_ref=rf_ref.at[:, 0], dst_ref=rfbuf.at[me_c, :, piece(j)], send_sem=plane_send.at[j],
            recv_sem=plane_recv.at[j], device_id=(me_c, j), device_id_type=MESH)

    for k in range(1, nf):
        plane_copy(k).start()

    inverse = 1.0 / math.sqrt(chans)

    def block_of(k):
        return lax.rem(me_c + k + nc, nc)

    def make_operator(block, offset, count):
        @pl.loop(0, count)
        def _(step):
            place = pl.ds(pl.multiple_of(block * cl + (offset + step) * 16, 16), 16)
            ex, ey, ez = elem[0, place, :], elem[1, place, :], elem[2, place, :]
            for base in range(0, vd, LANES):
                lanes = slice(base, base + LANES)
                vz = vox[2:3, lanes]
                dx, dy, dz = vox[0:1, lanes] - ex, vox[1:2, lanes] - ey, vz - ez
                square = dx * dx + dy * dy + dz * dz
                inv = lax.rsqrt(square)
                inv = inv * (1.5 - (0.5 * square) * (inv * inv))
                turns = wavenum * (vz + square * inv)
                turns = turns - ((turns + ROUND) - ROUND)
                z = turns * turns
                sine = turns * horner(SIN_POLY, z)
                cosine = horner(COS_POLY, z)
                weight = dz * inv * inverse
                twice = (weight + weight) * sine
                oper[0, place, lanes] = (weight - twice * sine).astype(BF16)
                oper[1, place, lanes] = (twice * cosine).astype(BF16)

    def multiply(block, first=False, last=False):
        place = pl.ds(pl.multiple_of(block * cl, cl), cl)
        real, imag = rfbuf[block, 0], rfbuf[block, 1]
        upper = jnp.concatenate([real, imag], axis=1)
        lower = jnp.concatenate([imag, -real], axis=1)
        width = min(256, vd)

        @pl.loop(0, vd // width)
        def _(step):
            lanes = pl.ds(pl.multiple_of(step * width, width), width)
            both = jnp.concatenate([oper[0, place, lanes], oper[1, place, lanes]], axis=0)
            for half, left in enumerate((upper, lower)):
                where = slice(half * frames, (half + 1) * frames)
                value = dot(left, both)
                if not first:
                    value = value + acc[where, lanes]
                if last:
                    vols[where, lanes] = value.astype(BF16)
                else:
                    acc[where, lanes] = value

    right = (lax.rem(me_c + 1, nc), me_f)
    left = (lax.rem(me_c + nc - 1, nc), me_f)
    steps = nc // 2

    def ring_copy(step, j, rightward, arriving):
        sign = -1 if rightward else 1
        block = block_of(sign * (step if arriving else step - 1))
        ref = rfbuf.at[block, :, piece(j)]
        if step == steps:
            ref = rfbuf.at[block, 0 if rightward else 1, piece(j)]
        sends, recvs = (right_send, right_recv) if rightward else (left_send, left_recv)
        index = (step - 1) * nf + j
        return pltpu.make_async_remote_copy(
            src_ref=ref, dst_ref=ref, send_sem=sends.at[index], recv_sem=recvs.at[index],
            device_id=right if rightward else left, device_id_type=MESH)

    stagger = share == 1 and nf % 2 == 0
    second = lax.rem(me_f, 2) == 1

    def unless_second(run):
        if stagger:
            pl.when(jnp.logical_not(second))(run)
        else:
            run()

    def send_own():
        for rightward in (True, False):
            ring_copy(1, me_f, rightward, False).start()

    def let_go():
        pl.semaphore_signal(go_sem, inc=1, device_id=(me_c, me_f + 1), device_id_type=MESH)

    unless_second(send_own)
    for load in loads:
        load.wait()
    vstart = pl.multiple_of(me_sub * vd, LANES)
    vox[...] = vox_ref[:, pl.ds(vstart, vd)].astype(F32)
    for axis in range(3):
        for base in range(0, chans, LANES):
            row = elem_ref[axis:axis + 1, base:base + LANES].astype(F32)
            elem[axis, base:base + LANES, :] = jnp.broadcast_to(row, (LANES, LANES)).T
    wavenum = (32.0 + sub_ref[me_bin].astype(F32)) / 64.0

    tall = cl // 16
    portion = 2 * tall // nf

    def portion_of_operator(phase, k):
        at = k * portion
        later = at >= tall
        block = jnp.where(later, block_of(-phase - 1), block_of(phase))
        make_operator(block, jnp.where(later, at - tall, at), portion)

    if stagger:
        @pl.when(second)
        def _():
            make_operator(0, 0, nc * tall)
            pl.semaphore_wait(go_sem, 1)
            send_own()

    unless_second(lambda: portion_of_operator(0, 0))

    @pl.loop(1, nf)
    def _(k):
        j = lax.rem(me_f - k + nf, nf)
        plane_arrival(j).wait_recv()
        for rightward in (True, False):
            ring_copy(1, j, rightward, False).start()
        unless_second(lambda: portion_of_operator(0, k))

    if stagger and steps == 1:
        unless_second(let_go)

    for step in range(1, steps):
        if step == 2:
            multiply(me_c, first=True)
        if step > 1:
            multiply(block_of(1 - step))
            multiply(block_of(step - 1))

        @pl.loop(0, nf)
        def _(k):
            j = lax.rem(me_f - k + nf, nf)
            for rightward in (True, False):
                ring_copy(step, j, rightward, True).wait_recv()
                ring_copy(step + 1, j, rightward, False).start()
            if stagger and step == steps - 1:
                @pl.when(jnp.logical_and(jnp.logical_not(second), k == GO_AT * nf // 8))
                def _():
                    let_go()

            unless_second(lambda: portion_of_operator(step, k))

    if steps <= 2:
        multiply(me_c, first=True)
    if steps > 1:
        multiply(block_of(1 - steps))
        multiply(block_of(steps - 1))

    @pl.loop(0, nf)
    def _(k):
        j = lax.rem(me_f - k + nf, nf)
        for rightward in (True, False):
            ring_copy(steps, j, rightward, True).wait_recv()

    multiply(block_of(steps), last=True)

    real, imag = vols[:frames, :], vols[frames:, :]
    both = jnp.concatenate([real, imag], axis=1)
    gram_re = dot_nt(both, both)
    gram_im = dot_nt(jnp.concatenate([real, -imag], axis=1), jnp.concatenate([imag, real], axis=1))
    across = lax.broadcasted_iota(jnp.int32, (frames, frames), 1)
    down = lax.broadcasted_iota(jnp.int32, (frames, frames), 0)
    part[...] = jnp.where(down <= across, gram_re, gram_im).astype(BF16)

    def slab_of(m):
        return pl.ds(pl.multiple_of(m * rows, rows), rows)

    def scatter(k):
        m, device = member(k)
        return pltpu.make_async_remote_copy(
            src_ref=part.at[slab_of(m)], dst_ref=slabs.at[me_g],
            send_sem=rs_send.at[m], recv_sem=rs_recv.at[me_g],
            device_id=device, device_id_type=MESH)

    def scatter_arrival(k):
        m, device = member(k)
        return pltpu.make_async_remote_copy(
            src_ref=part.at[slab_of(m)], dst_ref=slabs.at[m],
            send_sem=rs_send.at[m], recv_sem=rs_recv.at[m],
            device_id=device, device_id_type=MESH)

    def gather(k, arriving=False):
        m, device = member(k)
        source = m if arriving else me_g
        return pltpu.make_async_remote_copy(
            src_ref=total.at[slab_of(source)], dst_ref=total.at[slab_of(source)],
            send_sem=ag_send.at[m], recv_sem=ag_recv.at[source],
            device_id=device, device_id_type=MESH)

    for k in range(1, group):
        scatter(k).start()
    summed = part[slab_of(me_g), :].astype(F32)
    for k in range(1, group):
        scatter_arrival(k).wait_recv()
        summed = summed + slabs[member(k)[0]].astype(F32)
    total[slab_of(me_g), :] = summed.astype(BF16)
    for k in range(1, group):
        gather(k).start()
    for k in range(1, group):
        gather(k, True).wait_recv()

    packed = total[...].astype(F32)
    turned = packed.T
    mat_re = jnp.where(down <= across, packed, turned)
    mat_im = jnp.where(down > across, packed, jnp.where(down < across, -turned, 0.0))
    squares = jnp.sum(jnp.sum(mat_re * mat_re + mat_im * mat_im, axis=1, keepdims=True), axis=0, keepdims=True)
    factor = 4.0 / jnp.sqrt(squares + EPSILON)
    mat_re = mat_re * factor
    mat_im = mat_im * factor
    rhs = jnp.concatenate(
        [jnp.concatenate([mat_re, mat_im], axis=1), jnp.concatenate([-mat_im, mat_re], axis=1)], axis=0)
    rhs_high, rhs_low = split(rhs)

    def product(pair):
        high, low = split(pair)
        return dot(high, rhs_high) + (dot(high, rhs_low) + dot(low, rhs_high))

    first = jnp.concatenate([mat_re, mat_im], axis=1)
    second = product(first)
    third = product(second)
    poly = 0.3 * second - 0.03 * third - first
    acc[:frames, :frames] = jnp.where(down == across, 1.0, 0.0) + poly[:, :frames]
    acc[frames:, :frames] = poly[:, frames:]

    def out_copy(j):
        return pltpu.make_async_remote_copy(
            src_ref=sent.at[:, pl.ds(pl.multiple_of(j * fl, fl), fl)], dst_ref=out_ref.at[me_f],
            send_sem=out_send.at[j], recv_sem=out_recv.at[me_f],
            device_id=(me_c, j), device_id_type=MESH)

    chunks = 4
    per = nf // chunks
    height = per * fl
    my_chunk = me_f // per
    for step in range(1, chunks + 1):
        chunk = lax.rem(my_chunk + step, chunks)
        place = pl.ds(pl.multiple_of(chunk * height, height), height)
        below = pl.ds(pl.multiple_of(frames + chunk * height, height), height)
        h_re = acc[place, :frames].astype(BF16)
        h_im = acc[below, :frames].astype(BF16)
        lhs = jnp.concatenate(
            [jnp.concatenate([h_re, h_im], axis=1), jnp.concatenate([-h_im, h_re], axis=1)], axis=0)
        value = dot(lhs, vols[...]).astype(BF16)
        sent[0, place, :] = value[:height]
        sent[1, place, :] = value[height:]
        for q in range(per):
            j = chunk * per + q
            if step < chunks:
                out_copy(j).start()
            else:
                @pl.when(j != me_f)
                def _():
                    out_copy(j).start()
    own_out = pltpu.make_async_copy(sent.at[:, mine], out_ref.at[me_f], out_own)
    own_out.start()
    for k in range(1, nf):
        plane_copy(k).wait_send()
    for step in range(1, steps + 1):
        @pl.loop(0, nf)
        def _(j):
            for rightward in (True, False):
                ring_copy(step, j, rightward, False).wait_send()

    for k in range(1, group):
        scatter(k).wait_send()
        gather(k).wait_send()
    own_out.wait()
    for k in range(1, nf):
        j, device = planar(k)
        pltpu.make_async_remote_copy(
            src_ref=sent.at[:, mine], dst_ref=out_ref.at[j], send_sem=out_send.at[j],
            recv_sem=out_recv.at[j], device_id=device, device_id_type=MESH).wait()


def shards(nc, nf, rf_data, elem_pos, vox_pos, subbands):
    nbins, fl, cl = rf_data.shape[1:]
    frames = fl * nf
    chans = cl * nc
    share = nf // nbins
    vl = vox_pos.shape[1]
    vd = vl // share
    group = nc * share
    steps = nc // 2
    dma = pltpu.SemaphoreType.DMA
    received = pl.pallas_call(
        functools.partial(kernel, nc, nf, nbins),
        out_shape=jax.ShapeDtypeStruct((nf, 2, fl, vd), BF16),
        in_specs=[pl.BlockSpec(memory_space=pl.ANY)] * 4,
        out_specs=pl.BlockSpec(memory_space=pl.ANY),
        scratch_shapes=[
            pltpu.VMEM((nc, 2, frames, cl), BF16),
            pltpu.VMEM(elem_pos.shape, elem_pos.dtype),
            pltpu.VMEM(vox_pos.shape, vox_pos.dtype),
            pltpu.SMEM(subbands.shape, subbands.dtype),
            dma((3,)),
            pltpu.VMEM((3, chans, LANES), F32),
            pltpu.VMEM((3, vd), F32),
            pltpu.VMEM((2, chans, vd), BF16),
            pltpu.VMEM((2 * frames, vd), F32),
            pltpu.VMEM((2 * frames, vd), BF16),
            pltpu.VMEM((frames, frames), BF16),
            pltpu.VMEM((group, frames // group, frames), BF16),
            pltpu.VMEM((frames, frames), BF16),
            pltpu.VMEM((2, frames, vd), BF16),
            pltpu.SemaphoreType.REGULAR, dma, dma((nf,)), dma((nf,)),
            dma((steps * nf,)), dma((steps * nf,)), dma((steps * nf,)), dma((steps * nf,)),
            dma((group,)), dma((group,)), dma((group,)), dma((group,)),
            dma, dma((nf,)), dma((nf,)),
        ],
        compiler_params=pltpu.CompilerParams(
            collective_id=0, has_side_effects=True, vmem_limit_bytes=60 * 2**20),
    )(rf_data, elem_pos, vox_pos, subbands)
    received = received.reshape(nbins, share, 2, fl, vd)
    return jnp.transpose(received, (3, 2, 0, 1, 4)).reshape(fl, 2, nbins, vl)


def solution(mesh):
    return jax.shard_map(
        functools.partial(shards, mesh.shape["chan"], mesh.shape["frame"]),
        mesh=mesh,
        in_specs=(P(None, None, "frame", "chan"), P(), P(None, "chan"), P()),
        out_specs=P("frame", None, None, "chan"),
        check_vma=False,
    )
```
